32 devices in a mesh: snap: 2 (over x), row: 16 (over z, y, core).
Axes of the slice: x: 2, y: 2, z: 4, core: 2. Of those that a mesh axis runs over, the one named last changes fastest.
Arguments:
- snapshots: bfloat16 [256, 262144], P('snap', 'row'), may hold values from -64 to 64
- counts: int32 [16], P('row'), may hold values from 1 to 16384, 196608 in all
Outputs:
- basis: bfloat16 [256, 262144], P('snap', 'row')
- r_factor: float32 [256, 256], replicated
The draws below stay inside these ranges and needn't reach their ends.
Inputs may be any that keep to these rules, and one draw needn't show every extreme that they name: `counts`: at least one row and at most 16384 rows are live on each index of row, and some index has all 16384 live.
All inputs are finite; a program needn't handle non-finite values. No bound on the sum of `counts` on one device may be relied on, other than what follows from the above.
Results may differ from the reference program's by a relative error of at most 0.0049.
Values may be sent and summed in bfloat16 or wider, within the bound.
A program may use at most 64 MiB of HBM per device.

```python
import math
import jax
import jax.numpy as jnp
import numpy as np
from jax import lax

K = 256
ROWS_DEV = 16384
NROWS = 262144
N_ROW = 16


def draw_snapshots(key, part):
    keys = jax.random.split(key, 2)
    row_scale = jnp.exp(jax.random.uniform(keys[1], (1, NROWS), jnp.float32, 0.0, math.log(10.0)))
    base = jnp.clip(jax.random.normal(keys[0], (K, NROWS), jnp.float32), -5.0, 5.0)
    values = base * row_scale
    return values.astype(jnp.bfloat16)


def profile(number_of, total, limit, skew):
    portions = [(1 << 20) // math.isqrt(grade ** skew) + 1 for grade in range(2, number_of + 1)]
    rest, given = total - limit - (number_of - 1), [1] * (number_of - 1)
    while rest > 0:
        candidates = [i for i in range(number_of - 1) if given[i] < limit]
        mass, budget = sum([portions[i] for i in candidates]), rest
        for i in candidates:
            extra = min(limit - given[i], max(1, budget * portions[i] // mass), rest)
            given[i] = given[i] + extra
            rest = rest - extra
    return np.array([limit] + given)


def ragged(stream_key, amount, total, most, skew):
    if amount == 2:
        one = jax.random.randint(stream_key, (), max(1, total - most), min(most, total - 1) + 1)
        return jnp.stack([one, total - one])
    sizes = jnp.asarray(profile(amount, total, most, skew), jnp.int32)
    twos = (amount - 1) // 2
    source_of, receiver = sizes[1:1 + 2 * twos:2], sizes[2:2 + 2 * twos:2]
    room = jnp.minimum(source_of - 1, most - receiver)
    moved = jax.random.randint(jax.random.fold_in(stream_key, 1), (twos,), 0, 1 << 20) % (room + 1)
    sizes = sizes.at[1:1 + 2 * twos:2].set(source_of - moved).at[2:2 + 2 * twos:2].set(receiver + moved)
    return sizes[jax.random.permutation(jax.random.fold_in(stream_key, 2), amount)]


def setup_inputs(seed: int = 0) -> dict:
    splits = jax.random.split(jax.random.key(seed), 3)
    return {
        "snapshots": draw_snapshots(jax.random.fold_in(splits[2], 71), 0),
        "counts": ragged(splits[1], N_ROW, N_ROW * ROWS_DEV * 3 // 4, ROWS_DEV, 1).astype(jnp.int32),
    }


def reference(snapshots, counts):
    blocks = jnp.transpose(snapshots.reshape(K, N_ROW, ROWS_DEV), (1, 0, 2))
    slot = lax.broadcasted_iota(jnp.int32, (1, ROWS_DEV), 1)

    def masked(block, count):
        return jnp.where(slot < count, block, jnp.zeros_like(block))

    def add_gram(total, item):
        block, count = item
        live = masked(block, count)
        term = lax.dot_general(live.astype(jnp.float32), live.astype(jnp.float32), (((1,), (1,)), ((), ())), preferred_element_type=jnp.float32)
        return (total + term, 0)
    gram, _ = lax.scan(add_gram, jnp.zeros((K, K), jnp.float32), (blocks, counts))
    lower = jnp.linalg.cholesky(gram)
    scale = math.sqrt(NROWS)
    r_factor = lower.T / scale
    inverse = lax.linalg.triangular_solve(lower, jnp.eye(K, dtype=jnp.float32), left_side=True, lower=True).T
    weights = (inverse * scale).astype(jnp.bfloat16)

    def form(item):
        block, count = item
        live = masked(block, count)
        return lax.dot_general(weights.astype(jnp.float32), live.astype(jnp.float32), (((0,), (0,)), ((), ())), preferred_element_type=jnp.float32).astype(jnp.bfloat16)
    formed = lax.map(form, (blocks, counts))
    basis = jnp.transpose(formed, (1, 0, 2)).reshape(K, NROWS)
    return (basis, r_factor)
```

```python
import functools
import math

import jax
import jax.numpy as jnp
from jax import lax
from jax.experimental import pallas as pl
from jax.experimental.pallas import tpu as pltpu
from jax.sharding import PartitionSpec as P

MESH = pl.DeviceIdType.MESH
HIGH = lax.Precision.HIGHEST
LANES = 128
SUBLANES = 8


def gram_of(block):
    return lax.dot_general(
        block, block, (((1,), (1,)), ((), ())), preferred_element_type=jnp.float32
    )


def factors(gram, scale):
    lower = jnp.linalg.cholesky(gram)
    r_factor = lower.T / scale
    width = gram.shape[0]
    inverse = lax.linalg.triangular_solve(
        lower, jnp.eye(width, dtype=jnp.float32), left_side=True, lower=True
    ).T
    weights = (inverse * scale).astype(jnp.bfloat16)
    return (r_factor, weights)


def apply_weights(weights, block):
    return lax.dot_general(
        weights, block, (((0,), (0,)), ((), ())), preferred_element_type=jnp.float32
    ).astype(jnp.bfloat16)


def shards(snapshots, counts):
    narrow, slots = snapshots.shape
    slot = lax.broadcasted_iota(jnp.int32, (1, slots), 1)
    live = jnp.where(slot < counts[0], snapshots, jnp.zeros_like(snapshots))
    scale = math.sqrt(slots * lax.axis_size("row"))
    whole = lax.all_gather(live, "snap", axis=0, tiled=True)
    gram = lax.psum(gram_of(whole), "row")
    r_factor, weights = factors(gram, scale)
    start = lax.axis_index("snap") * narrow
    own_weights = lax.dynamic_slice_in_dim(weights, start, narrow, 1)
    basis = apply_weights(own_weights, whole)
    return (basis, r_factor)


def mxu_nt(a, b):
    return lax.dot_general(
        a, b, (((1,), (1,)), ((), ())), preferred_element_type=jnp.float32
    )


def partial_kernel(
    pieces, counts_ref, x_ref, part_ref, first_ref, later_ref,
    own, got, mine, theirs,
    load_sem, send_sem, recv_sem, keep_sem, back_sem, sum_send, sum_recv,
):
    snap = lax.axis_index("snap")
    other = {"snap": 1 - snap}
    narrow, slots = x_ref.shape
    half = slots // 2
    step = half // pieces
    count = counts_ref[0]

    barrier = pltpu.get_barrier_semaphore()
    pl.semaphore_signal(barrier, inc=1, device_id=other, device_id_type=MESH)

    loads = []
    for c in range(2 * pieces):
        at = pl.ds(c * step, step)
        copy = pltpu.make_async_copy(x_ref.at[:, at], own.at[:, at], load_sem.at[c])
        copy.start()
        loads.append(copy)

    pl.semaphore_wait(barrier, 1)
    sends = []
    for c in range(pieces):
        src = pl.ds(pl.multiple_of(snap * half + c * step, step), step)
        copy = pltpu.make_async_remote_copy(
            src_ref=x_ref.at[:, src],
            dst_ref=got.at[:, pl.ds(c * step, step)],
            send_sem=send_sem.at[c],
            recv_sem=recv_sem.at[c],
            device_id=other,
            device_id_type=MESH,
        )
        copy.start()
        sends.append(copy)

    def masked(block, start):
        lane = lax.broadcasted_iota(jnp.int32, block.shape, 1) + start
        return jnp.where(lane < count, block, jnp.zeros_like(block))

    total = jnp.zeros((narrow, narrow), jnp.float32)
    for c in range(2 * pieces):
        loads[c].wait()
        block = own[:, c * step:(c + 1) * step]
        total = total + mxu_nt(masked(block, c * step), block)
    mine[0] = total
    keep = pltpu.make_async_copy(own.at[:, pl.ds(half, half)], later_ref, keep_sem)
    keep.start()

    def sum_copy(i):
        return pltpu.make_async_remote_copy(
            src_ref=mine.at[i],
            dst_ref=theirs.at[i],
            send_sem=sum_send.at[i],
            recv_sem=sum_recv.at[i],
            device_id=other,
            device_id_type=MESH,
        )

    diagonal = sum_copy(0)
    diagonal.start()

    cross = jnp.zeros((narrow, narrow), jnp.float32)
    backs = []
    base = (1 - snap) * half
    for c in range(pieces):
        sends[c].wait_recv()
        here = pl.ds(c * step, step)
        back = pltpu.make_async_copy(got.at[:, here], first_ref.at[:, here], back_sem.at[c])
        back.start()
        backs.append(back)
        start = pl.multiple_of(base + c * step, step)
        block = masked(own[:, pl.ds(start, step)], start)
        cross = cross + mxu_nt(block, got[:, c * step:(c + 1) * step])
    mine[1] = jnp.where(snap == 0, cross, cross.T)
    crossed = sum_copy(1)
    crossed.start()
    for copy in sends:
        copy.wait_send()
    for copy in backs:
        copy.wait()
    keep.wait()
    diagonal.wait()
    low = jnp.where(snap == 0, mine[0], theirs[0])
    high = jnp.where(snap == 0, theirs[0], mine[0])
    part_ref[0:narrow, :] = low
    part_ref[narrow:2 * narrow, :] = high
    crossed.wait()
    part_ref[2 * narrow:3 * narrow, :] = mine[1] + theirs[1]


def partial_grams(snapshots, counts, pieces=8):
    narrow, slots = snapshots.shape
    half = slots // 2
    any_space = pl.BlockSpec(memory_space=pl.ANY)
    return pl.pallas_call(
        functools.partial(partial_kernel, pieces),
        name="partial_grams",
        out_shape=(
            jax.ShapeDtypeStruct((3 * narrow, narrow), jnp.float32),
            jax.ShapeDtypeStruct((narrow, half), snapshots.dtype),
            jax.ShapeDtypeStruct((narrow, half), snapshots.dtype),
        ),
        in_specs=[pl.BlockSpec(memory_space=pltpu.SMEM), any_space],
        out_specs=(pl.BlockSpec(memory_space=pltpu.VMEM), any_space, any_space),
        scratch_shapes=[
            pltpu.VMEM((narrow, slots), snapshots.dtype),
            pltpu.VMEM((narrow, half), snapshots.dtype),
            pltpu.VMEM((2, narrow, narrow), jnp.float32),
            pltpu.VMEM((2, narrow, narrow), jnp.float32),
            pltpu.SemaphoreType.DMA((2 * pieces,)),
            pltpu.SemaphoreType.DMA((pieces,)),
            pltpu.SemaphoreType.DMA((pieces,)),
            pltpu.SemaphoreType.DMA,
            pltpu.SemaphoreType.DMA((pieces,)),
            pltpu.SemaphoreType.DMA((2,)),
            pltpu.SemaphoreType.DMA((2,)),
        ],
        compiler_params=pltpu.CompilerParams(
            collective_id=0, has_side_effects=True, vmem_limit_bytes=24 << 20
        ),
    )(counts, snapshots)


def reduce_kernel(n, part_ref, out_ref, parts, send_sem, recv_sem, out_send, out_recv):
    me = lax.axis_index("row")
    rows = part_ref.shape[0] // n
    barrier = pltpu.get_barrier_semaphore()
    for d in range(1, n):
        peer = lax.rem(me + d, n)
        pl.semaphore_signal(barrier, inc=1, device_id={"row": peer}, device_id_type=MESH)
    pl.semaphore_wait(barrier, n - 1)

    def at(i):
        return pl.ds(pl.multiple_of(i * rows, SUBLANES), rows)

    copies = []
    for d in range(1, n):
        peer = lax.rem(me + d, n)
        copy = pltpu.make_async_remote_copy(
            src_ref=part_ref.at[at(peer)],
            dst_ref=parts.at[d - 1],
            send_sem=send_sem.at[d - 1],
            recv_sem=recv_sem.at[d - 1],
            device_id={"row": peer},
            device_id_type=MESH,
        )
        copy.start()
        copies.append(copy)
    total = part_ref[at(me), :]
    for d in range(1, n):
        copies[d - 1].wait_recv()
        total = total + parts[d - 1]
    out_ref[at(me), :] = total
    results = []
    for d in range(1, n):
        peer = lax.rem(me + d, n)
        copy = pltpu.make_async_remote_copy(
            src_ref=out_ref.at[at(me)],
            dst_ref=out_ref.at[at(me)],
            send_sem=out_send.at[d - 1],
            recv_sem=out_recv.at[d - 1],
            device_id={"row": peer},
            device_id_type=MESH,
        )
        copy.start()
        results.append(copy)
    for copy in copies:
        copy.wait_send()
    for copy in results:
        copy.wait()


def reduce_rows(part):
    n = lax.axis_size("row")
    rows = part.shape[0] // n
    vmem = pl.BlockSpec(memory_space=pltpu.VMEM)
    return pl.pallas_call(
        functools.partial(reduce_kernel, n),
        name="reduce_rows",
        out_shape=jax.ShapeDtypeStruct(part.shape, part.dtype),
        in_specs=[vmem],
        out_specs=vmem,
        scratch_shapes=[
            pltpu.VMEM((n - 1, rows, part.shape[1]), part.dtype),
            pltpu.SemaphoreType.DMA((n - 1,)),
            pltpu.SemaphoreType.DMA((n - 1,)),
            pltpu.SemaphoreType.DMA((n - 1,)),
            pltpu.SemaphoreType.DMA((n - 1,)),
        ],
        compiler_params=pltpu.CompilerParams(
            collective_id=1, has_side_effects=True, vmem_limit_bytes=8 << 20
        ),
        cost_estimate=pl.CostEstimate(
            flops=1 << 30, bytes_accessed=48 << 20, transcendentals=0
        ),
    )(part)


def eliminate(groups):
    shape = groups[0].shape
    width = shape[1]
    lane = lax.broadcasted_iota(jnp.int32, shape, 1)
    sub = lax.broadcasted_iota(jnp.int32, shape, 0)
    groups = list(groups)
    for j in range(width):
        g, p = divmod(j, shape[0])
        here = lane == j
        columns = [
            jnp.broadcast_to(groups[v][:, j:j + 1], shape) for v in range(g, len(groups))
        ]
        pivot = jnp.broadcast_to(columns[0][p:p + 1, :], shape)
        root = lax.rsqrt(pivot)
        root = root * (1.5 - 0.5 * pivot * root * root)
        row = jnp.broadcast_to(groups[g][p:p + 1, :], shape)
        row = jnp.where(here, root, row * root)
        for v in range(g, len(groups)):
            left = jnp.where(here, 0.0, groups[v]) - (columns[v - g] * root) * row
            if v == g:
                left = jnp.where(sub == p, row, jnp.where(sub > p, left, groups[v]))
            groups[v] = left
    return groups


def factor_kernel(scale, gram_ref, r_ref, own_ref, other_ref, work, roots):
    narrow = gram_ref.shape[1]
    snap = lax.axis_index("snap")
    row = lax.broadcasted_iota(jnp.int32, (narrow, narrow), 0)
    col = lax.broadcasted_iota(jnp.int32, (narrow, narrow), 1)

    def dot(a, b, dims):
        return lax.dot_general(
            a, b, (dims, ((), ())), precision=HIGH, preferred_element_type=jnp.float32
        )

    def diagonal(which):
        full = work[which]
        inverse = jnp.where(col <= row, full, 0.0)
        upper = jnp.where(col > row, full, 0.0)
        upper = jnp.where(col == row, 1.0 / full, upper)
        return inverse, upper

    work[0] = gram_ref[0:narrow, :]
    work[1] = gram_ref[narrow:2 * narrow, :]

    @pl.loop(0, 2)
    def _(block):
        groups = [
            work[block, SUBLANES * v:SUBLANES * (v + 1), :] for v in range(narrow // SUBLANES)
        ]
        for v, group in enumerate(eliminate(groups)):
            work[block, SUBLANES * v:SUBLANES * (v + 1), :] = group

        @pl.when(block == 0)
        def _():
            inverse, _ = diagonal(0)
            right = dot(inverse, gram_ref[2 * narrow:3 * narrow, :], ((1,), (0,)))
            roots[...] = right
            work[1] = work[1] - dot(right, right, ((0,), (0,)))

    inverse0, upper0 = diagonal(0)
    inverse1, upper1 = diagonal(1)
    right = roots[...]
    below = -dot(inverse1, dot(right, inverse0, ((0,), (0,))), ((1,), (0,)))
    r_ref[0:narrow, 0:narrow] = upper0 / scale
    r_ref[0:narrow, narrow:] = right / scale
    r_ref[narrow:, 0:narrow] = jnp.zeros_like(right)
    r_ref[narrow:, narrow:] = upper1 / scale
    own = jnp.where(snap == 0, inverse0, inverse1)
    own_ref[...] = (own * scale).astype(own_ref.dtype)
    other = jnp.where(snap == 0, 0.0, below)
    other_ref[...] = (other * scale).astype(other_ref.dtype)


def factor(gram, scale, dtype):
    narrow = gram.shape[1]
    vmem = pl.BlockSpec(memory_space=pltpu.VMEM)
    return pl.pallas_call(
        functools.partial(factor_kernel, scale),
        name="factor",
        out_shape=(
            jax.ShapeDtypeStruct((2 * narrow, 2 * narrow), jnp.float32),
            jax.ShapeDtypeStruct((narrow, narrow), dtype),
            jax.ShapeDtypeStruct((narrow, narrow), dtype),
        ),
        in_specs=[vmem],
        out_specs=(vmem, vmem, vmem),
        scratch_shapes=[
            pltpu.VMEM((2, narrow, narrow), jnp.float32),
            pltpu.VMEM((narrow, narrow), jnp.float32),
        ],
        compiler_params=pltpu.CompilerParams(vmem_limit_bytes=8 << 20),
        cost_estimate=pl.CostEstimate(
            flops=1 << 30, bytes_accessed=96 << 20, transcendentals=0
        ),
    )(gram)


def basis_kernel(parts, counts_ref, own_w, other_w, own_ref, first_ref, later_ref, out_ref):
    c = pl.program_id(0)
    width = out_ref.shape[1]
    got = jnp.where(c < parts // 2, first_ref[...], later_ref[...])
    value = lax.dot_general(
        own_w[...], own_ref[...], (((1,), (0,)), ((), ())), preferred_element_type=jnp.float32
    ) + lax.dot_general(
        other_w[...], got, (((1,), (0,)), ((), ())), preferred_element_type=jnp.float32
    )
    lane = lax.broadcasted_iota(jnp.int32, out_ref.shape, 1) + c * width
    out_ref[...] = jnp.where(lane < counts_ref[0], value, 0.0).astype(out_ref.dtype)


def form_basis(counts, own_w, other_w, snapshots, first, later, parts=8):
    narrow, slots = snapshots.shape
    width = slots // parts
    mid = parts // 2
    small = pl.BlockSpec((narrow, narrow), lambda c: (0, 0))
    return pl.pallas_call(
        functools.partial(basis_kernel, parts),
        name="form_basis",
        grid=(parts,),
        out_shape=jax.ShapeDtypeStruct(snapshots.shape, snapshots.dtype),
        in_specs=[
            pl.BlockSpec(memory_space=pltpu.SMEM),
            small,
            small,
            pl.BlockSpec((narrow, width), lambda c: (0, c)),
            pl.BlockSpec((narrow, width), lambda c: (0, jnp.minimum(c, mid - 1))),
            pl.BlockSpec((narrow, width), lambda c: (0, jnp.maximum(c - mid, 0))),
        ],
        out_specs=pl.BlockSpec((narrow, width), lambda c: (0, c)),
        compiler_params=pltpu.CompilerParams(vmem_limit_bytes=16 << 20),
    )(counts, own_w, other_w, snapshots, first, later)


def halves(snapshots, counts):
    slots = snapshots.shape[1]
    scale = math.sqrt(slots * lax.axis_size("row"))
    part, first, later = partial_grams(snapshots, counts)
    later = lax.ppermute(later, "snap", [(0, 1)])
    gram = reduce_rows(part)
    r_factor, own_w, other_w = factor(gram, scale, snapshots.dtype)
    basis = form_basis(counts, own_w, other_w, snapshots, first, later)
    return (basis, r_factor)


def two_halves(mesh):
    return mesh.shape["snap"] == 2 and mesh.shape["row"] == 16


def solution(mesh):
    placed = (P("snap", "row"), P("row"))
    body = halves if two_halves(mesh) else shards
    return jax.shard_map(
        body, mesh=mesh, in_specs=placed, out_specs=(P("snap", "row"), P()), check_vma=False
    )
```

```python
import functools
import math

import jax
import jax.numpy as jnp
from jax import lax
from jax.experimental import pallas as pl
from jax.experimental.pallas import tpu as pltpu
from jax.sharding import PartitionSpec as P

MESH = pl.DeviceIdType.MESH
HIGH = lax.Precision.HIGHEST
LANES = 128
SUBLANES = 8


def gram_of(block):
    return lax.dot_general(
        block, block, (((1,), (1,)), ((), ())), preferred_element_type=jnp.float32
    )


def factors(gram, scale):
    lower = jnp.linalg.cholesky(gram)
    r_factor = lower.T / scale
    width = gram.shape[0]
    inverse = lax.linalg.triangular_solve(
        lower, jnp.eye(width, dtype=jnp.float32), left_side=True, lower=True
    ).T
    weights = (inverse * scale).astype(jnp.bfloat16)
    return (r_factor, weights)


def apply_weights(weights, block):
    return lax.dot_general(
        weights, block, (((0,), (0,)), ((), ())), preferred_element_type=jnp.float32
    ).astype(jnp.bfloat16)


def shards(snapshots, counts):
    narrow, slots = snapshots.shape
    slot = lax.broadcasted_iota(jnp.int32, (1, slots), 1)
    live = jnp.where(slot < counts[0], snapshots, jnp.zeros_like(snapshots))
    scale = math.sqrt(slots * lax.axis_size("row"))
    whole = lax.all_gather(live, "snap", axis=0, tiled=True)
    gram = lax.psum(gram_of(whole), "row")
    r_factor, weights = factors(gram, scale)
    start = lax.axis_index("snap") * narrow
    own_weights = lax.dynamic_slice_in_dim(weights, start, narrow, 1)
    basis = apply_weights(own_weights, whole)
    return (basis, r_factor)


def mxu_nt(a, b):
    return lax.dot_general(
        a, b, (((1,), (1,)), ((), ())), preferred_element_type=jnp.float32
    )


def partial_kernel(
    pieces, counts_ref, x_ref, part_ref, first_ref, later_ref,
    own, got, mine, theirs,
    load_sem, send_sem, recv_sem, keep_sem, back_sem, sum_send, sum_recv,
):
    snap = lax.axis_index("snap")
    other = {"snap": 1 - snap}
    narrow, slots = x_ref.shape
    half = slots // 2
    step = half // pieces
    count = counts_ref[0]

    barrier = pltpu.get_barrier_semaphore()
    pl.semaphore_signal(barrier, inc=1, device_id=other, device_id_type=MESH)

    loads = []
    for c in range(2 * pieces):
        at = pl.ds(c * step, step)
        copy = pltpu.make_async_copy(x_ref.at[:, at], own.at[:, at], load_sem.at[c])
        copy.start()
        loads.append(copy)

    pl.semaphore_wait(barrier, 1)
    sends = []
    for c in range(pieces):
        src = pl.ds(pl.multiple_of(snap * half + c * step, step), step)
        copy = pltpu.make_async_remote_copy(
            src_ref=x_ref.at[:, src],
            dst_ref=got.at[:, pl.ds(c * step, step)],
            send_sem=send_sem.at[c],
            recv_sem=recv_sem.at[c],
            device_id=other,
            device_id_type=MESH,
        )
        copy.start()
        sends.append(copy)

    def masked(block, start):
        lane = lax.broadcasted_iota(jnp.int32, block.shape, 1) + start
        return jnp.where(lane < count, block, jnp.zeros_like(block))

    total = jnp.zeros((narrow, narrow), jnp.float32)
    for c in range(2 * pieces):
        loads[c].wait()
        block = own[:, c * step:(c + 1) * step]
        total = total + mxu_nt(masked(block, c * step), block)
    mine[0] = total
    keep = pltpu.make_async_copy(own.at[:, pl.ds(half, half)], later_ref, keep_sem)
    keep.start()

    def sum_copy(i):
        return pltpu.make_async_remote_copy(
            src_ref=mine.at[i],
            dst_ref=theirs.at[i],
            send_sem=sum_send.at[i],
            recv_sem=sum_recv.at[i],
            device_id=other,
            device_id_type=MESH,
        )

    diagonal = sum_copy(0)
    diagonal.start()

    cross = jnp.zeros((narrow, narrow), jnp.float32)
    backs = []
    base = (1 - snap) * half
    for c in range(pieces):
        sends[c].wait_recv()
        here = pl.ds(c * step, step)
        back = pltpu.make_async_copy(got.at[:, here], first_ref.at[:, here], back_sem.at[c])
        back.start()
        backs.append(back)
        start = pl.multiple_of(base + c * step, step)
        block = masked(own[:, pl.ds(start, step)], start)
        cross = cross + mxu_nt(block, got[:, c * step:(c + 1) * step])
    mine[1] = jnp.where(snap == 0, cross, cross.T)
    crossed = sum_copy(1)
    crossed.start()
    for copy in sends:
        copy.wait_send()
    for copy in backs:
        copy.wait()
    keep.wait()
    diagonal.wait()
    low = jnp.where(snap == 0, mine[0], theirs[0])
    high = jnp.where(snap == 0, theirs[0], mine[0])
    part_ref[0:narrow, :] = low
    part_ref[narrow:2 * narrow, :] = high
    crossed.wait()
    part_ref[2 * narrow:3 * narrow, :] = mine[1] + theirs[1]


def partial_grams(snapshots, counts, pieces=8):
    narrow, slots = snapshots.shape
    half = slots // 2
    any_space = pl.BlockSpec(memory_space=pl.ANY)
    return pl.pallas_call(
        functools.partial(partial_kernel, pieces),
        name="partial_grams",
        out_shape=(
            jax.ShapeDtypeStruct((3 * narrow, narrow), jnp.float32),
            jax.ShapeDtypeStruct((narrow, half), snapshots.dtype),
            jax.ShapeDtypeStruct((narrow, half), snapshots.dtype),
        ),
        in_specs=[
            pl.BlockSpec(memory_space=pltpu.SMEM),
            pl.BlockSpec(memory_space=pltpu.HBM),
        ],
        out_specs=(pl.BlockSpec(memory_space=pltpu.VMEM), any_space, any_space),
        scratch_shapes=[
            pltpu.VMEM((narrow, slots), snapshots.dtype),
            pltpu.VMEM((narrow, half), snapshots.dtype),
            pltpu.VMEM((2, narrow, narrow), jnp.float32),
            pltpu.VMEM((2, narrow, narrow), jnp.float32),
            pltpu.SemaphoreType.DMA((2 * pieces,)),
            pltpu.SemaphoreType.DMA((pieces,)),
            pltpu.SemaphoreType.DMA((pieces,)),
            pltpu.SemaphoreType.DMA,
            pltpu.SemaphoreType.DMA((pieces,)),
            pltpu.SemaphoreType.DMA((2,)),
            pltpu.SemaphoreType.DMA((2,)),
        ],
        compiler_params=pltpu.CompilerParams(
            collective_id=0, has_side_effects=True, vmem_limit_bytes=62 << 20
        ),
    )(counts, snapshots)


def reduce_kernel(n, part_ref, out_ref, parts, send_sem, recv_sem, out_send, out_recv):
    me = lax.axis_index("row")
    rows = part_ref.shape[0] // n
    barrier = pltpu.get_barrier_semaphore()
    for d in range(1, n):
        peer = lax.rem(me + d, n)
        pl.semaphore_signal(barrier, inc=1, device_id={"row": peer}, device_id_type=MESH)
    pl.semaphore_wait(barrier, n - 1)

    def at(i):
        return pl.ds(pl.multiple_of(i * rows, SUBLANES), rows)

    copies = []
    for d in range(1, n):
        peer = lax.rem(me + d, n)
        copy = pltpu.make_async_remote_copy(
            src_ref=part_ref.at[at(peer)],
            dst_ref=parts.at[d - 1],
            send_sem=send_sem.at[d - 1],
            recv_sem=recv_sem.at[d - 1],
            device_id={"row": peer},
            device_id_type=MESH,
        )
        copy.start()
        copies.append(copy)
    total = part_ref[at(me), :]
    for d in range(1, n):
        copies[d - 1].wait_recv()
        total = total + parts[d - 1]
    out_ref[at(me), :] = total
    results = []
    for d in range(1, n):
        peer = lax.rem(me + d, n)
        copy = pltpu.make_async_remote_copy(
            src_ref=out_ref.at[at(me)],
            dst_ref=out_ref.at[at(me)],
            send_sem=out_send.at[d - 1],
            recv_sem=out_recv.at[d - 1],
            device_id={"row": peer},
            device_id_type=MESH,
        )
        copy.start()
        results.append(copy)
    for copy in copies:
        copy.wait_send()
    for copy in results:
        copy.wait()


def reduce_rows(part):
    n = lax.axis_size("row")
    rows = part.shape[0] // n
    vmem = pl.BlockSpec(memory_space=pltpu.VMEM)
    return pl.pallas_call(
        functools.partial(reduce_kernel, n),
        name="reduce_rows",
        out_shape=jax.ShapeDtypeStruct(part.shape, part.dtype),
        in_specs=[vmem],
        out_specs=vmem,
        scratch_shapes=[
            pltpu.VMEM((n - 1, rows, part.shape[1]), part.dtype),
            pltpu.SemaphoreType.DMA((n - 1,)),
            pltpu.SemaphoreType.DMA((n - 1,)),
            pltpu.SemaphoreType.DMA((n - 1,)),
            pltpu.SemaphoreType.DMA((n - 1,)),
        ],
        compiler_params=pltpu.CompilerParams(
            collective_id=1, has_side_effects=True, vmem_limit_bytes=8 << 20
        ),
        cost_estimate=pl.CostEstimate(
            flops=1 << 30, bytes_accessed=48 << 20, transcendentals=0
        ),
    )(part)


def eliminate(groups):
    shape = groups[0].shape
    tall = shape[0]
    lane = lax.broadcasted_iota(jnp.int32, shape, 1)
    sub = lax.broadcasted_iota(jnp.int32, shape, 0)
    groups = list(groups)
    count = len(groups)

    def line(block, p):
        return jnp.broadcast_to(block[p:p + 1, :], shape)

    for g in range(count):
        columns = [
            [
                jnp.broadcast_to(groups[v][:, g * tall + q:g * tall + q + 1], shape)
                for v in range(g, count)
            ]
            for q in range(tall)
        ]
        for p in range(tall):
            here = lane == g * tall + p
            pivot = line(columns[p][0], p)
            root = lax.rsqrt(pivot)
            root = root * (1.5 - 0.5 * pivot * root * root)
            lefts = [column * root for column in columns[p]]
            lefts[0] = jnp.where(sub > p, lefts[0], 0.0)
            for q in range(p + 1, tall):
                top = line(columns[q][0], p) * root
                columns[q] = [c - m * top for c, m in zip(columns[q], lefts)]
            row = jnp.where(here, root, line(groups[g], p) * root)
            for v in range(g, count):
                old = groups[v]
                new = jnp.where(here, 0.0, old) - lefts[v - g] * row
                if v == g:
                    new = jnp.where(sub == p, row, jnp.where(sub > p, new, old))
                groups[v] = new
    return groups


def factor_kernel(scale, gram_ref, r_ref, own_ref, other_ref, work, roots):
    narrow = gram_ref.shape[1]
    snap = lax.axis_index("snap")
    row = lax.broadcasted_iota(jnp.int32, (narrow, narrow), 0)
    col = lax.broadcasted_iota(jnp.int32, (narrow, narrow), 1)

    def dot(a, b, dims):
        return lax.dot_general(
            a, b, (dims, ((), ())), precision=HIGH, preferred_element_type=jnp.float32
        )

    def diagonal(which):
        full = work[which]
        inverse = jnp.where(col <= row, full, 0.0)
        upper = jnp.where(col > row, full, 0.0)
        upper = jnp.where(col == row, 1.0 / full, upper)
        return inverse, upper

    work[0] = gram_ref[0:narrow, :]
    work[1] = gram_ref[narrow:2 * narrow, :]

    @pl.loop(0, 2)
    def _(block):
        groups = [
            work[block, SUBLANES * v:SUBLANES * (v + 1), :] for v in range(narrow // SUBLANES)
        ]
        for v, group in enumerate(eliminate(groups)):
            work[block, SUBLANES * v:SUBLANES * (v + 1), :] = group

        @pl.when(block == 0)
        def _():
            inverse, _ = diagonal(0)
            right = dot(inverse, gram_ref[2 * narrow:3 * narrow, :], ((1,), (0,)))
            roots[...] = right
            work[1] = work[1] - dot(right, right, ((0,), (0,)))

    inverse0, upper0 = diagonal(0)
    inverse1, upper1 = diagonal(1)
    right = roots[...]
    below = -dot(inverse1, dot(right, inverse0, ((0,), (0,))), ((1,), (0,)))
    r_ref[0:narrow, 0:narrow] = upper0 / scale
    r_ref[0:narrow, narrow:] = right / scale
    r_ref[narrow:, 0:narrow] = jnp.zeros_like(right)
    r_ref[narrow:, narrow:] = upper1 / scale
    own = jnp.where(snap == 0, inverse0, inverse1)
    own_ref[...] = (own * scale).astype(own_ref.dtype)
    other = jnp.where(snap == 0, 0.0, below)
    other_ref[...] = (other * scale).astype(other_ref.dtype)


def factor(gram, scale, dtype):
    narrow = gram.shape[1]
    vmem = pl.BlockSpec(memory_space=pltpu.VMEM)
    return pl.pallas_call(
        functools.partial(factor_kernel, scale),
        name="factor",
        out_shape=(
            jax.ShapeDtypeStruct((2 * narrow, 2 * narrow), jnp.float32),
            jax.ShapeDtypeStruct((narrow, narrow), dtype),
            jax.ShapeDtypeStruct((narrow, narrow), dtype),
        ),
        in_specs=[vmem],
        out_specs=(vmem, vmem, vmem),
        scratch_shapes=[
            pltpu.VMEM((2, narrow, narrow), jnp.float32),
            pltpu.VMEM((narrow, narrow), jnp.float32),
        ],
        compiler_params=pltpu.CompilerParams(vmem_limit_bytes=8 << 20),
        cost_estimate=pl.CostEstimate(
            flops=1 << 30, bytes_accessed=96 << 20, transcendentals=0
        ),
    )(gram)


def basis_kernel(
    pieces, first_piece, counts_ref, own_w, other_w, own_ref, got_ref, *rest
):
    out_ref, stage, sems = rest[-3:]
    narrow, width = got_ref.shape
    step = width // pieces
    count = counts_ref[0]
    weights = jnp.concatenate([own_w[...], other_w[...]], axis=1)
    copies = []
    for c in range(pieces):
        here = pl.ds(c * step, step)
        start = first_piece + c * step
        both = jnp.concatenate(
            [own_ref[:, start:start + step], got_ref[:, c * step:(c + 1) * step]], axis=0
        )
        value = lax.dot_general(
            weights, both, (((1,), (0,)), ((), ())), preferred_element_type=jnp.float32
        )
        lane = lax.broadcasted_iota(jnp.int32, value.shape, 1) + start
        stage[:, c * step:(c + 1) * step] = jnp.where(lane < count, value, 0.0).astype(stage.dtype)
        copy = pltpu.make_async_copy(
            stage.at[:, here], out_ref.at[:, pl.ds(start, step)], sems.at[c]
        )
        copy.start()
        copies.append(copy)
    for copy in copies:
        copy.wait()


def form_basis(counts, own_w, other_w, snapshots, got, start, before=None, pieces=4):
    narrow, width = got.shape
    vmem = pl.BlockSpec(memory_space=pltpu.VMEM)
    hbm = pl.BlockSpec(memory_space=pltpu.HBM)
    operands = [counts, own_w, other_w, snapshots, got]
    specs = [pl.BlockSpec(memory_space=pltpu.SMEM), vmem, vmem, vmem, vmem]
    aliases = {}
    if before is not None:
        aliases = {len(operands): 0}
        operands.append(before)
        specs.append(hbm)
    return pl.pallas_call(
        functools.partial(basis_kernel, pieces, start),
        name="form_basis",
        out_shape=jax.ShapeDtypeStruct(snapshots.shape, snapshots.dtype),
        in_specs=specs,
        out_specs=hbm,
        input_output_aliases=aliases,
        scratch_shapes=[
            pltpu.VMEM((narrow, width), snapshots.dtype),
            pltpu.SemaphoreType.DMA((pieces,)),
        ],
        compiler_params=pltpu.CompilerParams(vmem_limit_bytes=16 << 20),
        cost_estimate=pl.CostEstimate(
            flops=4 * narrow * narrow * width,
            bytes_accessed=8 * narrow * width,
            transcendentals=0,
        ),
    )(*operands)


def halves(snapshots, counts):
    slots = snapshots.shape[1]
    scale = math.sqrt(slots * lax.axis_size("row"))
    part, first, later = partial_grams(snapshots, counts)
    later = lax.ppermute(later, "snap", [(0, 1)])
    gram = reduce_rows(part)
    r_factor, own_w, other_w = factor(gram, scale, snapshots.dtype)
    half = snapshots.shape[1] // 2
    basis = form_basis(counts, own_w, other_w, snapshots, first, 0)
    basis = form_basis(counts, own_w, other_w, snapshots, later, half, basis)
    return (basis, r_factor)


def two_halves(mesh):
    return mesh.shape["snap"] == 2 and mesh.shape["row"] == 16


def solution(mesh):
    placed = (P("snap", "row"), P("row"))
    body = halves if two_halves(mesh) else shards
    return jax.shard_map(
        body, mesh=mesh, in_specs=placed, out_specs=(P("snap", "row"), P()), check_vma=False
    )
```

```python
import functools
import math

import jax
import jax.numpy as jnp
from jax import lax
from jax.experimental import pallas as pl
from jax.experimental.pallas import tpu as pltpu
from jax.sharding import PartitionSpec as P

MESH = pl.DeviceIdType.MESH
HIGH = lax.Precision.HIGHEST
LANES = 128
SUBLANES = 8


def gram_of(block):
    return lax.dot_general(
        block, block, (((1,), (1,)), ((), ())), preferred_element_type=jnp.float32
    )


def factors(gram, scale):
    lower = jnp.linalg.cholesky(gram)
    r_factor = lower.T / scale
    width = gram.shape[0]
    inverse = lax.linalg.triangular_solve(
        lower, jnp.eye(width, dtype=jnp.float32), left_side=True, lower=True
    ).T
    weights = (inverse * scale).astype(jnp.bfloat16)
    return (r_factor, weights)


def apply_weights(weights, block):
    return lax.dot_general(
        weights, block, (((0,), (0,)), ((), ())), preferred_element_type=jnp.float32
    ).astype(jnp.bfloat16)


def shards(snapshots, counts):
    narrow, slots = snapshots.shape
    slot = lax.broadcasted_iota(jnp.int32, (1, slots), 1)
    live = jnp.where(slot < counts[0], snapshots, jnp.zeros_like(snapshots))
    scale = math.sqrt(slots * lax.axis_size("row"))
    whole = lax.all_gather(live, "snap", axis=0, tiled=True)
    gram = lax.psum(gram_of(whole), "row")
    r_factor, weights = factors(gram, scale)
    start = lax.axis_index("snap") * narrow
    own_weights = lax.dynamic_slice_in_dim(weights, start, narrow, 1)
    basis = apply_weights(own_weights, whole)
    return (basis, r_factor)


def mxu_nt(a, b):
    return lax.dot_general(
        a, b, (((1,), (1,)), ((), ())), preferred_element_type=jnp.float32
    )


def partial_kernel(
    pieces, counts_ref, x_ref, part_ref, first_ref, later_ref, last_ref,
    own, got, mine, theirs,
    load_sem, send_sem, recv_sem, keep_sem, back_sem, sum_send, sum_recv,
):
    snap = lax.axis_index("snap")
    other = {"snap": 1 - snap}
    narrow, slots = x_ref.shape
    half = slots // 2
    step = half // pieces
    count = counts_ref[0]

    barrier = pltpu.get_barrier_semaphore()
    pl.semaphore_signal(barrier, inc=1, device_id=other, device_id_type=MESH)

    loads = []
    for c in range(2 * pieces):
        at = pl.ds(c * step, step)
        copy = pltpu.make_async_copy(x_ref.at[:, at], own.at[:, at], load_sem.at[c])
        copy.start()
        loads.append(copy)

    pl.semaphore_wait(barrier, 1)

    def send(i, src, dst, size):
        copy = pltpu.make_async_remote_copy(
            src_ref=x_ref.at[:, pl.ds(src, size)],
            dst_ref=got.at[:, pl.ds(dst, size)],
            send_sem=send_sem.at[i],
            recv_sem=recv_sem.at[i],
            device_id=other,
            device_id_type=MESH,
        )
        copy.start()
        return copy

    sends = [
        send(c, pl.multiple_of(snap * half + c * step, step), c * step, step)
        for c in range(pieces)
    ]

    def masked(block, start):
        lane = lax.broadcasted_iota(jnp.int32, block.shape, 1) + start
        return jnp.where(lane < count, block, jnp.zeros_like(block))

    total = jnp.zeros((narrow, narrow), jnp.float32)
    for c in range(2 * pieces):
        loads[c].wait()
        block = own[:, c * step:(c + 1) * step]
        total = total + mxu_nt(masked(block, c * step), block)
    mine[0] = total
    keeps = []
    start = first_ref.shape[1]
    for i, ref in enumerate((later_ref, last_ref)):
        size = ref.shape[1]
        keep = pltpu.make_async_copy(own.at[:, pl.ds(start, size)], ref, keep_sem.at[i])
        keep.start()
        keeps.append(keep)
        start += size

    def sum_copy(i):
        return pltpu.make_async_remote_copy(
            src_ref=mine.at[i],
            dst_ref=theirs.at[i],
            send_sem=sum_send.at[i],
            recv_sem=sum_recv.at[i],
            device_id=other,
            device_id_type=MESH,
        )

    diagonal = sum_copy(0)
    diagonal.start()
    ahead = (first_ref.shape[1] - half) // 2
    extras = [send(pieces, half, half, ahead)]

    cross = jnp.zeros((narrow, narrow), jnp.float32)
    backs = []
    base = (1 - snap) * half
    for c in range(pieces):
        sends[c].wait_recv()
        here = pl.ds(c * step, step)
        back = pltpu.make_async_copy(got.at[:, here], first_ref.at[:, here], back_sem.at[c])
        back.start()
        backs.append(back)
        start = pl.multiple_of(base + c * step, step)
        block = masked(own[:, pl.ds(start, step)], start)
        cross = cross + mxu_nt(block, got[:, c * step:(c + 1) * step])
    mine[1] = jnp.where(snap == 0, cross, cross.T)
    crossed = sum_copy(1)
    crossed.start()
    extras.append(send(pieces + 1, half + ahead, half + ahead, ahead))
    for copy in sends:
        copy.wait_send()
    for copy in keeps:
        copy.wait()
    diagonal.wait()
    low = jnp.where(snap == 0, mine[0], theirs[0])
    high = jnp.where(snap == 0, theirs[0], mine[0])
    part_ref[0:narrow, :] = low
    part_ref[narrow:2 * narrow, :] = high
    crossed.wait()
    part_ref[2 * narrow:3 * narrow, :] = mine[1] + theirs[1]
    for i, copy in enumerate(extras):
        copy.wait()
        here = pl.ds(half + i * ahead, ahead)
        back = pltpu.make_async_copy(
            got.at[:, here], first_ref.at[:, here], back_sem.at[pieces + i]
        )
        back.start()
        backs.append(back)
    for copy in backs:
        copy.wait()


def partial_grams(snapshots, counts, pieces=8):
    narrow, slots = snapshots.shape
    half = slots // 2
    step = half // pieces
    early = half + step
    last = 2 * step
    later = slots - early - last
    any_space = pl.BlockSpec(memory_space=pl.ANY)
    return pl.pallas_call(
        functools.partial(partial_kernel, pieces),
        name="partial_grams",
        out_shape=(
            jax.ShapeDtypeStruct((3 * narrow, narrow), jnp.float32),
            jax.ShapeDtypeStruct((narrow, early), snapshots.dtype),
            jax.ShapeDtypeStruct((narrow, later), snapshots.dtype),
            jax.ShapeDtypeStruct((narrow, last), snapshots.dtype),
        ),
        in_specs=[
            pl.BlockSpec(memory_space=pltpu.SMEM),
            pl.BlockSpec(memory_space=pltpu.HBM),
        ],
        out_specs=(pl.BlockSpec(memory_space=pltpu.VMEM), any_space, any_space, any_space),
        scratch_shapes=[
            pltpu.VMEM((narrow, slots), snapshots.dtype),
            pltpu.VMEM((narrow, early), snapshots.dtype),
            pltpu.VMEM((2, narrow, narrow), jnp.float32),
            pltpu.VMEM((2, narrow, narrow), jnp.float32),
            pltpu.SemaphoreType.DMA((2 * pieces,)),
            pltpu.SemaphoreType.DMA((pieces + 2,)),
            pltpu.SemaphoreType.DMA((pieces + 2,)),
            pltpu.SemaphoreType.DMA((2,)),
            pltpu.SemaphoreType.DMA((pieces + 2,)),
            pltpu.SemaphoreType.DMA((2,)),
            pltpu.SemaphoreType.DMA((2,)),
        ],
        compiler_params=pltpu.CompilerParams(
            collective_id=0, has_side_effects=True, vmem_limit_bytes=62 << 20
        ),
    )(counts, snapshots)


def reduce_kernel(n, part_ref, out_ref, parts, send_sem, recv_sem, out_send, out_recv):
    me = lax.axis_index("row")
    rows = part_ref.shape[0] // n
    barrier = pltpu.get_barrier_semaphore()
    for d in range(1, n):
        peer = lax.rem(me + d, n)
        pl.semaphore_signal(barrier, inc=1, device_id={"row": peer}, device_id_type=MESH)
    pl.semaphore_wait(barrier, n - 1)

    def at(i):
        return pl.ds(pl.multiple_of(i * rows, SUBLANES), rows)

    copies = []
    for d in range(1, n):
        peer = lax.rem(me + d, n)
        copy = pltpu.make_async_remote_copy(
            src_ref=part_ref.at[at(peer)],
            dst_ref=parts.at[d - 1],
            send_sem=send_sem.at[d - 1],
            recv_sem=recv_sem.at[d - 1],
            device_id={"row": peer},
            device_id_type=MESH,
        )
        copy.start()
        copies.append(copy)
    total = part_ref[at(me), :]
    for d in range(1, n):
        copies[d - 1].wait_recv()
        total = total + parts[d - 1]
    out_ref[at(me), :] = total
    results = []
    for d in range(1, n):
        peer = lax.rem(me + d, n)
        copy = pltpu.make_async_remote_copy(
            src_ref=out_ref.at[at(me)],
            dst_ref=out_ref.at[at(me)],
            send_sem=out_send.at[d - 1],
            recv_sem=out_recv.at[d - 1],
            device_id={"row": peer},
            device_id_type=MESH,
        )
        copy.start()
        results.append(copy)
    for copy in copies:
        copy.wait_send()
    for copy in results:
        copy.wait()


def reduce_rows(part):
    n = lax.axis_size("row")
    rows = part.shape[0] // n
    vmem = pl.BlockSpec(memory_space=pltpu.VMEM)
    return pl.pallas_call(
        functools.partial(reduce_kernel, n),
        name="reduce_rows",
        out_shape=jax.ShapeDtypeStruct(part.shape, part.dtype),
        in_specs=[vmem],
        out_specs=vmem,
        scratch_shapes=[
            pltpu.VMEM((n - 1, rows, part.shape[1]), part.dtype),
            pltpu.SemaphoreType.DMA((n - 1,)),
            pltpu.SemaphoreType.DMA((n - 1,)),
            pltpu.SemaphoreType.DMA((n - 1,)),
            pltpu.SemaphoreType.DMA((n - 1,)),
        ],
        compiler_params=pltpu.CompilerParams(
            collective_id=1, has_side_effects=True, vmem_limit_bytes=8 << 20
        ),
        cost_estimate=pl.CostEstimate(
            flops=1 << 30, bytes_accessed=48 << 20, transcendentals=0
        ),
    )(part)


def eliminate(groups):
    shape = groups[0].shape
    tall = shape[0]
    lane = lax.broadcasted_iota(jnp.int32, shape, 1)
    sub = lax.broadcasted_iota(jnp.int32, shape, 0)
    groups = list(groups)
    count = len(groups)

    def line(block, p):
        return jnp.broadcast_to(block[p:p + 1, :], shape)

    for g in range(count):
        columns = [
            [
                jnp.broadcast_to(groups[v][:, g * tall + q:g * tall + q + 1], shape)
                for v in range(g, count)
            ]
            for q in range(tall)
        ]
        for p in range(tall):
            here = lane == g * tall + p
            pivot = line(columns[p][0], p)
            root = lax.rsqrt(pivot)
            root = root * (1.5 - 0.5 * pivot * root * root)
            lefts = [column * root for column in columns[p]]
            lefts[0] = jnp.where(sub > p, lefts[0], 0.0)
            for q in range(p + 1, tall):
                top = line(columns[q][0], p) * root
                columns[q] = [c - m * top for c, m in zip(columns[q], lefts)]
            row = jnp.where(here, root, line(groups[g], p) * root)
            for v in range(g, count):
                old = groups[v]
                new = jnp.where(here, 0.0, old) - lefts[v - g] * row
                if v == g:
                    new = jnp.where(sub == p, row, jnp.where(sub > p, new, old))
                groups[v] = new
    return groups


def factor_kernel(scale, gram_ref, r_ref, own_ref, other_ref, work, roots):
    narrow = gram_ref.shape[1]
    snap = lax.axis_index("snap")
    row = lax.broadcasted_iota(jnp.int32, (narrow, narrow), 0)
    col = lax.broadcasted_iota(jnp.int32, (narrow, narrow), 1)

    def dot(a, b, dims):
        return lax.dot_general(
            a, b, (dims, ((), ())), precision=HIGH, preferred_element_type=jnp.float32
        )

    def diagonal(which):
        full = work[which]
        inverse = jnp.where(col <= row, full, 0.0)
        upper = jnp.where(col > row, full, 0.0)
        upper = jnp.where(col == row, 1.0 / full, upper)
        return inverse, upper

    work[0] = gram_ref[0:narrow, :]
    work[1] = gram_ref[narrow:2 * narrow, :]

    @pl.loop(0, 2)
    def _(block):
        groups = [
            work[block, SUBLANES * v:SUBLANES * (v + 1), :] for v in range(narrow // SUBLANES)
        ]
        for v, group in enumerate(eliminate(groups)):
            work[block, SUBLANES * v:SUBLANES * (v + 1), :] = group

        @pl.when(block == 0)
        def _():
            inverse, _ = diagonal(0)
            right = dot(inverse, gram_ref[2 * narrow:3 * narrow, :], ((1,), (0,)))
            roots[...] = right
            work[1] = work[1] - dot(right, right, ((0,), (0,)))

    inverse0, upper0 = diagonal(0)
    inverse1, upper1 = diagonal(1)
    right = roots[...]
    below = -dot(inverse1, dot(right, inverse0, ((0,), (0,))), ((1,), (0,)))
    r_ref[0:narrow, 0:narrow] = upper0 / scale
    r_ref[0:narrow, narrow:] = right / scale
    r_ref[narrow:, 0:narrow] = jnp.zeros_like(right)
    r_ref[narrow:, narrow:] = upper1 / scale
    own = jnp.where(snap == 0, inverse0, inverse1)
    own_ref[...] = (own * scale).astype(own_ref.dtype)
    other = jnp.where(snap == 0, 0.0, below)
    other_ref[...] = (other * scale).astype(other_ref.dtype)


def factor(gram, scale, dtype):
    narrow = gram.shape[1]
    vmem = pl.BlockSpec(memory_space=pltpu.VMEM)
    return pl.pallas_call(
        functools.partial(factor_kernel, scale),
        name="factor",
        out_shape=(
            jax.ShapeDtypeStruct((2 * narrow, 2 * narrow), jnp.float32),
            jax.ShapeDtypeStruct((narrow, narrow), dtype),
            jax.ShapeDtypeStruct((narrow, narrow), dtype),
        ),
        in_specs=[vmem],
        out_specs=(vmem, vmem, vmem),
        scratch_shapes=[
            pltpu.VMEM((2, narrow, narrow), jnp.float32),
            pltpu.VMEM((narrow, narrow), jnp.float32),
        ],
        compiler_params=pltpu.CompilerParams(vmem_limit_bytes=8 << 20),
        cost_estimate=pl.CostEstimate(
            flops=1 << 30, bytes_accessed=96 << 20, transcendentals=0
        ),
    )(gram)


def basis_kernel(
    pieces, first_piece, counts_ref, own_w, other_w, own_ref, got_ref, *rest
):
    out_ref, stage, sems = rest[-3:]
    narrow, width = got_ref.shape
    step = width // pieces
    count = counts_ref[0]
    weights = jnp.concatenate([own_w[...], other_w[...]], axis=1)
    copies = []
    for c in range(pieces):
        here = pl.ds(c * step, step)
        start = first_piece + c * step
        both = jnp.concatenate(
            [own_ref[:, start:start + step], got_ref[:, c * step:(c + 1) * step]], axis=0
        )
        value = lax.dot_general(
            weights, both, (((1,), (0,)), ((), ())), preferred_element_type=jnp.float32
        )
        lane = lax.broadcasted_iota(jnp.int32, value.shape, 1) + start
        stage[:, c * step:(c + 1) * step] = jnp.where(lane < count, value, 0.0).astype(stage.dtype)
        copy = pltpu.make_async_copy(
            stage.at[:, here], out_ref.at[:, pl.ds(start, step)], sems.at[c]
        )
        copy.start()
        copies.append(copy)
    for copy in copies:
        copy.wait()


def form_basis(counts, own_w, other_w, snapshots, got, start, before=None, most=2048):
    narrow, width = got.shape
    pieces = next(n for n in range(1, width) if width % (n * LANES) == 0 and width // n <= most)
    vmem = pl.BlockSpec(memory_space=pltpu.VMEM)
    hbm = pl.BlockSpec(memory_space=pltpu.HBM)
    operands = [counts, own_w, other_w, snapshots, got]
    specs = [pl.BlockSpec(memory_space=pltpu.SMEM), vmem, vmem, vmem, vmem]
    aliases = {}
    if before is not None:
        aliases = {len(operands): 0}
        operands.append(before)
        specs.append(hbm)
    return pl.pallas_call(
        functools.partial(basis_kernel, pieces, start),
        name="form_basis",
        out_shape=jax.ShapeDtypeStruct(snapshots.shape, snapshots.dtype),
        in_specs=specs,
        out_specs=hbm,
        input_output_aliases=aliases,
        scratch_shapes=[
            pltpu.VMEM((narrow, width), snapshots.dtype),
            pltpu.SemaphoreType.DMA((pieces,)),
        ],
        compiler_params=pltpu.CompilerParams(vmem_limit_bytes=16 << 20),
        cost_estimate=pl.CostEstimate(
            flops=4 * narrow * narrow * width,
            bytes_accessed=8 * narrow * width,
            transcendentals=0,
        ),
    )(*operands)


def halves(snapshots, counts):
    slots = snapshots.shape[1]
    scale = math.sqrt(slots * lax.axis_size("row"))
    part, *got = partial_grams(snapshots, counts)
    got[1:] = [lax.ppermute(piece, "snap", [(0, 1)]) for piece in got[1:]]
    gram = reduce_rows(part)
    r_factor, own_w, other_w = factor(gram, scale, snapshots.dtype)
    basis, start = None, 0
    for piece in got:
        basis = form_basis(counts, own_w, other_w, snapshots, piece, start, basis)
        start += piece.shape[1]
    return (basis, r_factor)


def two_halves(mesh):
    return mesh.shape["snap"] == 2 and mesh.shape["row"] == 16


def solution(mesh):
    placed = (P("snap", "row"), P("row"))
    body = halves if two_halves(mesh) else shards
    return jax.shard_map(
        body, mesh=mesh, in_specs=placed, out_specs=(P("snap", "row"), P()), check_vma=False
    )
```

```python
import functools
import math

import jax
import jax.numpy as jnp
from jax import lax
from jax.experimental import pallas as pl
from jax.experimental.pallas import tpu as pltpu
from jax.sharding import PartitionSpec as P

MESH = pl.DeviceIdType.MESH
HIGH = lax.Precision.HIGHEST
LANES = 128
SUBLANES = 8


def gram_of(block):
    return lax.dot_general(
        block, block, (((1,), (1,)), ((), ())), preferred_element_type=jnp.float32
    )


def factors(gram, scale):
    lower = jnp.linalg.cholesky(gram)
    r_factor = lower.T / scale
    width = gram.shape[0]
    inverse = lax.linalg.triangular_solve(
        lower, jnp.eye(width, dtype=jnp.float32), left_side=True, lower=True
    ).T
    weights = (inverse * scale).astype(jnp.bfloat16)
    return (r_factor, weights)


def apply_weights(weights, block):
    return lax.dot_general(
        weights, block, (((0,), (0,)), ((), ())), preferred_element_type=jnp.float32
    ).astype(jnp.bfloat16)


def shards(snapshots, counts):
    narrow, slots = snapshots.shape
    slot = lax.broadcasted_iota(jnp.int32, (1, slots), 1)
    live = jnp.where(slot < counts[0], snapshots, jnp.zeros_like(snapshots))
    scale = math.sqrt(slots * lax.axis_size("row"))
    whole = lax.all_gather(live, "snap", axis=0, tiled=True)
    gram = lax.psum(gram_of(whole), "row")
    r_factor, weights = factors(gram, scale)
    start = lax.axis_index("snap") * narrow
    own_weights = lax.dynamic_slice_in_dim(weights, start, narrow, 1)
    basis = apply_weights(own_weights, whole)
    return (basis, r_factor)


def mxu_nt(a, b):
    return lax.dot_general(
        a, b, (((1,), (1,)), ((), ())), preferred_element_type=jnp.float32
    )


def partial_kernel(
    pieces, counts_ref, x_ref, part_ref, first_ref, later_ref, last_ref,
    own, got, mine, near, summed, theirs,
    load_sem, send_sem, recv_sem, keep_sem, back_sem, sum_send, sum_recv, near_send, near_recv,
):
    snap = lax.axis_index("snap")
    core = lax.rem(lax.axis_index("row"), 2)
    other = {"snap": 1 - snap}
    pair = {"row": lax.axis_index("row") + 1 - 2 * core}
    narrow, slots = x_ref.shape
    half = slots // 2
    step = half // pieces
    count = counts_ref[0]

    barrier = pltpu.get_barrier_semaphore()
    pl.semaphore_signal(barrier, inc=1, device_id=other, device_id_type=MESH)
    pl.semaphore_signal(barrier, inc=1, device_id=pair, device_id_type=MESH)

    loads = []
    for c in range(2 * pieces):
        at = pl.ds(c * step, step)
        copy = pltpu.make_async_copy(x_ref.at[:, at], own.at[:, at], load_sem.at[c])
        copy.start()
        loads.append(copy)

    pl.semaphore_wait(barrier, 2)

    def send(i, src, dst, size):
        copy = pltpu.make_async_remote_copy(
            src_ref=x_ref.at[:, pl.ds(src, size)],
            dst_ref=got.at[:, pl.ds(dst, size)],
            send_sem=send_sem.at[i],
            recv_sem=recv_sem.at[i],
            device_id=other,
            device_id_type=MESH,
        )
        copy.start()
        return copy

    sends = [
        send(c, pl.multiple_of(snap * half + c * step, step), c * step, step)
        for c in range(pieces)
    ]

    def masked(block, start):
        lane = lax.broadcasted_iota(jnp.int32, block.shape, 1) + start
        return jnp.where(lane < count, block, jnp.zeros_like(block))

    total = jnp.zeros((narrow, narrow), jnp.float32)
    for c in range(2 * pieces):
        loads[c].wait()
        block = own[:, c * step:(c + 1) * step]
        total = total + mxu_nt(masked(block, c * step), block)
    mine[0] = total
    keeps = []
    start = first_ref.shape[1]
    for i, ref in enumerate((later_ref, last_ref)):
        size = ref.shape[1]
        keep = pltpu.make_async_copy(own.at[:, pl.ds(start, size)], ref, keep_sem.at[i])
        keep.start()
        keeps.append(keep)
        start += size

    rows = narrow // 2

    def sum_copy(i):
        away = pltpu.make_async_remote_copy(
            src_ref=mine.at[i, pl.ds(pl.multiple_of((1 - core) * rows, SUBLANES), rows)],
            dst_ref=near.at[i],
            send_sem=near_send.at[i],
            recv_sem=near_recv.at[i],
            device_id=pair,
            device_id_type=MESH,
        )
        away.start()
        away.wait()
        kept = mine[i, pl.ds(pl.multiple_of(core * rows, SUBLANES), rows), :]
        summed[i] = kept + near[i]
        return pltpu.make_async_remote_copy(
            src_ref=summed.at[i],
            dst_ref=theirs.at[i],
            send_sem=sum_send.at[i],
            recv_sem=sum_recv.at[i],
            device_id=other,
            device_id_type=MESH,
        )

    diagonal = sum_copy(0)
    diagonal.start()
    spare = first_ref.shape[1] - half
    ahead = spare * 3 // 4
    extras = [send(pieces, half, half, ahead)]

    cross = jnp.zeros((narrow, narrow), jnp.float32)
    backs = []
    base = (1 - snap) * half
    for c in range(pieces):
        sends[c].wait_recv()
        here = pl.ds(c * step, step)
        back = pltpu.make_async_copy(got.at[:, here], first_ref.at[:, here], back_sem.at[c])
        back.start()
        backs.append(back)
        start = pl.multiple_of(base + c * step, step)
        block = masked(own[:, pl.ds(start, step)], start)
        cross = cross + mxu_nt(block, got[:, c * step:(c + 1) * step])
    mine[1] = jnp.where(snap == 0, cross, cross.T)
    crossed = sum_copy(1)
    crossed.start()
    extras.append(send(pieces + 1, half + ahead, half + ahead, spare - ahead))
    for copy in sends:
        copy.wait_send()
    for copy in keeps:
        copy.wait()
    diagonal.wait()
    part_ref[0:rows, :] = jnp.where(snap == 0, summed[0], theirs[0])
    part_ref[rows:2 * rows, :] = jnp.where(snap == 0, theirs[0], summed[0])
    crossed.wait()
    part_ref[2 * rows:3 * rows, :] = summed[1] + theirs[1]
    for i, (copy, at, size) in enumerate(
        zip(extras, (half, half + ahead), (ahead, spare - ahead))
    ):
        copy.wait()
        here = pl.ds(at, size)
        back = pltpu.make_async_copy(
            got.at[:, here], first_ref.at[:, here], back_sem.at[pieces + i]
        )
        back.start()
        backs.append(back)
    for copy in backs:
        copy.wait()


def partial_grams(snapshots, counts, pieces=8):
    narrow, slots = snapshots.shape
    half = slots // 2
    step = half // pieces
    early = half + step
    last = 2 * step
    later = slots - early - last
    any_space = pl.BlockSpec(memory_space=pl.ANY)
    return pl.pallas_call(
        functools.partial(partial_kernel, pieces),
        name="partial_grams",
        out_shape=(
            jax.ShapeDtypeStruct((3 * narrow // 2, narrow), jnp.float32),
            jax.ShapeDtypeStruct((narrow, early), snapshots.dtype),
            jax.ShapeDtypeStruct((narrow, later), snapshots.dtype),
            jax.ShapeDtypeStruct((narrow, last), snapshots.dtype),
        ),
        in_specs=[
            pl.BlockSpec(memory_space=pltpu.SMEM),
            pl.BlockSpec(memory_space=pltpu.HBM),
        ],
        out_specs=(pl.BlockSpec(memory_space=pltpu.VMEM), any_space, any_space, any_space),
        scratch_shapes=[
            pltpu.VMEM((narrow, slots), snapshots.dtype),
            pltpu.VMEM((narrow, early), snapshots.dtype),
            pltpu.VMEM((2, narrow, narrow), jnp.float32),
            pltpu.VMEM((2, narrow // 2, narrow), jnp.float32),
            pltpu.VMEM((2, narrow // 2, narrow), jnp.float32),
            pltpu.VMEM((2, narrow // 2, narrow), jnp.float32),
            pltpu.SemaphoreType.DMA((2 * pieces,)),
            pltpu.SemaphoreType.DMA((pieces + 2,)),
            pltpu.SemaphoreType.DMA((pieces + 2,)),
            pltpu.SemaphoreType.DMA((2,)),
            pltpu.SemaphoreType.DMA((pieces + 2,)),
            pltpu.SemaphoreType.DMA((2,)),
            pltpu.SemaphoreType.DMA((2,)),
            pltpu.SemaphoreType.DMA((2,)),
            pltpu.SemaphoreType.DMA((2,)),
        ],
        compiler_params=pltpu.CompilerParams(
            collective_id=0, has_side_effects=True, vmem_limit_bytes=62 << 20
        ),
    )(counts, snapshots)


def reduce_kernel(n, part_ref, out_ref, parts, send_sem, recv_sem, out_send, out_recv):
    me = lax.axis_index("row")
    core, chip = lax.rem(me, 2), lax.div(me, 2)
    chips = n // 2
    rows = part_ref.shape[0] // chips
    barrier = pltpu.get_barrier_semaphore()
    for d in range(1, n):
        peer = lax.rem(me + d, n)
        pl.semaphore_signal(barrier, inc=1, device_id={"row": peer}, device_id_type=MESH)
    pl.semaphore_wait(barrier, n - 1)

    def at(i):
        return pl.ds(pl.multiple_of(i * rows, SUBLANES), rows)

    copies = []
    for d in range(1, chips):
        peer = lax.rem(chip + d, chips)
        copy = pltpu.make_async_remote_copy(
            src_ref=part_ref.at[at(peer)],
            dst_ref=parts.at[d - 1],
            send_sem=send_sem.at[d - 1],
            recv_sem=recv_sem.at[d - 1],
            device_id={"row": 2 * peer + core},
            device_id_type=MESH,
        )
        copy.start()
        copies.append(copy)
    total = part_ref[at(chip), :]
    for d in range(1, chips):
        copies[d - 1].wait_recv()
        total = total + parts[d - 1]
    out_ref[core, at(chip), :] = total
    results = []
    for d in range(1, n):
        peer = lax.rem(me + d, n)
        copy = pltpu.make_async_remote_copy(
            src_ref=out_ref.at[core, at(chip)],
            dst_ref=out_ref.at[core, at(chip)],
            send_sem=out_send.at[d - 1],
            recv_sem=out_recv.at[d - 1],
            device_id={"row": peer},
            device_id_type=MESH,
        )
        copy.start()
        results.append(copy)
    for copy in copies:
        copy.wait_send()
    for copy in results:
        copy.wait()


def reduce_rows(part):
    n = lax.axis_size("row")
    chips = n // 2
    rows = part.shape[0] // chips
    vmem = pl.BlockSpec(memory_space=pltpu.VMEM)
    return pl.pallas_call(
        functools.partial(reduce_kernel, n),
        name="reduce_rows",
        out_shape=jax.ShapeDtypeStruct((2, *part.shape), part.dtype),
        in_specs=[vmem],
        out_specs=vmem,
        scratch_shapes=[
            pltpu.VMEM((chips - 1, rows, part.shape[1]), part.dtype),
            pltpu.SemaphoreType.DMA((chips - 1,)),
            pltpu.SemaphoreType.DMA((chips - 1,)),
            pltpu.SemaphoreType.DMA((n - 1,)),
            pltpu.SemaphoreType.DMA((n - 1,)),
        ],
        compiler_params=pltpu.CompilerParams(
            collective_id=1, has_side_effects=True, vmem_limit_bytes=8 << 20
        ),
        cost_estimate=pl.CostEstimate(
            flops=1 << 30, bytes_accessed=48 << 20, transcendentals=0
        ),
    )(part)


def eliminate(groups):
    shape = groups[0].shape
    tall = shape[0]
    lane = lax.broadcasted_iota(jnp.int32, shape, 1)
    sub = lax.broadcasted_iota(jnp.int32, shape, 0)
    groups = list(groups)
    count = len(groups)

    def line(block, p):
        return jnp.broadcast_to(block[p:p + 1, :], shape)

    for g in range(count):
        columns = [
            [
                jnp.broadcast_to(groups[v][:, g * tall + q:g * tall + q + 1], shape)
                for v in range(g, count)
            ]
            for q in range(tall)
        ]
        for p in range(tall):
            here = lane == g * tall + p
            pivot = line(columns[p][0], p)
            root = lax.rsqrt(pivot)
            root = root * (1.5 - 0.5 * pivot * root * root)
            lefts = [column * root for column in columns[p]]
            lefts[0] = jnp.where(sub > p, lefts[0], 0.0)
            for q in range(p + 1, tall):
                top = line(columns[q][0], p) * root
                columns[q] = [c - m * top for c, m in zip(columns[q], lefts)]
            row = jnp.where(here, root, line(groups[g], p) * root)
            for v in range(g, count):
                old = groups[v]
                new = jnp.where(here, 0.0, old) - lefts[v - g] * row
                if v == g:
                    new = jnp.where(sub == p, row, jnp.where(sub > p, new, old))
                groups[v] = new
    return groups


def factor_kernel(scale, gram_ref, r_ref, own_ref, other_ref, work, roots):
    narrow = gram_ref.shape[2]
    rows = narrow // 2
    snap = lax.axis_index("snap")
    row = lax.broadcasted_iota(jnp.int32, (narrow, narrow), 0)
    col = lax.broadcasted_iota(jnp.int32, (narrow, narrow), 1)

    def gram(i):
        here = slice(i * rows, (i + 1) * rows)
        return jnp.concatenate([gram_ref[0, here, :], gram_ref[1, here, :]], axis=0)

    def dot(a, b, dims):
        return lax.dot_general(
            a, b, (dims, ((), ())), precision=HIGH, preferred_element_type=jnp.float32
        )

    def diagonal(which):
        full = work[which]
        inverse = jnp.where(col <= row, full, 0.0)
        upper = jnp.where(col > row, full, 0.0)
        upper = jnp.where(col == row, 1.0 / full, upper)
        return inverse, upper

    work[0] = gram(0)
    work[1] = gram(1)

    @pl.loop(0, 2)
    def _(block):
        groups = [
            work[block, SUBLANES * v:SUBLANES * (v + 1), :] for v in range(narrow // SUBLANES)
        ]
        for v, group in enumerate(eliminate(groups)):
            work[block, SUBLANES * v:SUBLANES * (v + 1), :] = group

        @pl.when(block == 0)
        def _():
            inverse, _ = diagonal(0)
            right = dot(inverse, gram(2), ((1,), (0,)))
            roots[...] = right
            work[1] = work[1] - dot(right, right, ((0,), (0,)))

    inverse0, upper0 = diagonal(0)
    inverse1, upper1 = diagonal(1)
    right = roots[...]
    below = -dot(inverse1, dot(right, inverse0, ((0,), (0,))), ((1,), (0,)))
    r_ref[0:narrow, 0:narrow] = upper0 / scale
    r_ref[0:narrow, narrow:] = right / scale
    r_ref[narrow:, 0:narrow] = jnp.zeros_like(right)
    r_ref[narrow:, narrow:] = upper1 / scale
    own = jnp.where(snap == 0, inverse0, inverse1)
    own_ref[...] = (own * scale).astype(own_ref.dtype)
    other = jnp.where(snap == 0, 0.0, below)
    other_ref[...] = (other * scale).astype(other_ref.dtype)


def factor(gram, scale, dtype):
    narrow = gram.shape[2]
    vmem = pl.BlockSpec(memory_space=pltpu.VMEM)
    return pl.pallas_call(
        functools.partial(factor_kernel, scale),
        name="factor",
        out_shape=(
            jax.ShapeDtypeStruct((2 * narrow, 2 * narrow), jnp.float32),
            jax.ShapeDtypeStruct((narrow, narrow), dtype),
            jax.ShapeDtypeStruct((narrow, narrow), dtype),
        ),
        in_specs=[vmem],
        out_specs=(vmem, vmem, vmem),
        scratch_shapes=[
            pltpu.VMEM((2, narrow, narrow), jnp.float32),
            pltpu.VMEM((narrow, narrow), jnp.float32),
        ],
        compiler_params=pltpu.CompilerParams(vmem_limit_bytes=8 << 20),
        cost_estimate=pl.CostEstimate(
            flops=1 << 30, bytes_accessed=96 << 20, transcendentals=0
        ),
    )(gram)


def basis_kernel(
    pieces, first_piece, counts_ref, own_w, other_w, own_ref, got_ref, *rest
):
    out_ref, stage, sems = rest[-3:]
    narrow, width = got_ref.shape
    step = width // pieces
    count = counts_ref[0]
    weights = jnp.concatenate([own_w[...], other_w[...]], axis=1)
    copies = []
    for c in range(pieces):
        here = pl.ds(c * step, step)
        start = first_piece + c * step
        both = jnp.concatenate(
            [own_ref[:, start:start + step], got_ref[:, c * step:(c + 1) * step]], axis=0
        )
        value = lax.dot_general(
            weights, both, (((1,), (0,)), ((), ())), preferred_element_type=jnp.float32
        )
        lane = lax.broadcasted_iota(jnp.int32, value.shape, 1) + start
        stage[:, c * step:(c + 1) * step] = jnp.where(lane < count, value, 0.0).astype(stage.dtype)
        copy = pltpu.make_async_copy(
            stage.at[:, here], out_ref.at[:, pl.ds(start, step)], sems.at[c]
        )
        copy.start()
        copies.append(copy)
    for copy in copies:
        copy.wait()


def form_basis(counts, own_w, other_w, snapshots, got, start, before=None, most=2048):
    narrow, width = got.shape
    pieces = next(n for n in range(1, width) if width % (n * LANES) == 0 and width // n <= most)
    vmem = pl.BlockSpec(memory_space=pltpu.VMEM)
    hbm = pl.BlockSpec(memory_space=pltpu.HBM)
    operands = [counts, own_w, other_w, snapshots, got]
    specs = [pl.BlockSpec(memory_space=pltpu.SMEM), vmem, vmem, vmem, vmem]
    aliases = {}
    if before is not None:
        aliases = {len(operands): 0}
        operands.append(before)
        specs.append(hbm)
    return pl.pallas_call(
        functools.partial(basis_kernel, pieces, start),
        name="form_basis",
        out_shape=jax.ShapeDtypeStruct(snapshots.shape, snapshots.dtype),
        in_specs=specs,
        out_specs=hbm,
        input_output_aliases=aliases,
        scratch_shapes=[
            pltpu.VMEM((narrow, width), snapshots.dtype),
            pltpu.SemaphoreType.DMA((pieces,)),
        ],
        compiler_params=pltpu.CompilerParams(vmem_limit_bytes=16 << 20),
        cost_estimate=pl.CostEstimate(
            flops=4 * narrow * narrow * width,
            bytes_accessed=8 * narrow * width,
            transcendentals=0,
        ),
    )(*operands)


def halves(snapshots, counts):
    slots = snapshots.shape[1]
    scale = math.sqrt(slots * lax.axis_size("row"))
    part, *got = partial_grams(snapshots, counts)
    got[1:] = [lax.ppermute(piece, "snap", [(0, 1)]) for piece in got[1:]]
    gram = reduce_rows(part)
    r_factor, own_w, other_w = factor(gram, scale, snapshots.dtype)
    basis, start = None, 0
    for piece in got:
        basis = form_basis(counts, own_w, other_w, snapshots, piece, start, basis)
        start += piece.shape[1]
    return (basis, r_factor)


def two_halves(mesh):
    return mesh.shape["snap"] == 2 and mesh.shape["row"] == 16


def solution(mesh):
    placed = (P("snap", "row"), P("row"))
    body = halves if two_halves(mesh) else shards
    return jax.shard_map(
        body, mesh=mesh, in_specs=placed, out_specs=(P("snap", "row"), P()), check_vma=False
    )
```

```python
import functools
import math

import jax
import jax.numpy as jnp
from jax import lax
from jax.experimental import pallas as pl
from jax.experimental.pallas import tpu as pltpu
from jax.sharding import PartitionSpec as P

MESH = pl.DeviceIdType.MESH
HIGH = lax.Precision.HIGHEST
LANES = 128
SUBLANES = 8


def gram_of(block):
    return lax.dot_general(
        block, block, (((1,), (1,)), ((), ())), preferred_element_type=jnp.float32
    )


def factors(gram, scale):
    lower = jnp.linalg.cholesky(gram)
    r_factor = lower.T / scale
    width = gram.shape[0]
    inverse = lax.linalg.triangular_solve(
        lower, jnp.eye(width, dtype=jnp.float32), left_side=True, lower=True
    ).T
    weights = (inverse * scale).astype(jnp.bfloat16)
    return (r_factor, weights)


def apply_weights(weights, block):
    return lax.dot_general(
        weights, block, (((0,), (0,)), ((), ())), preferred_element_type=jnp.float32
    ).astype(jnp.bfloat16)


def shards(snapshots, counts):
    narrow, slots = snapshots.shape
    slot = lax.broadcasted_iota(jnp.int32, (1, slots), 1)
    live = jnp.where(slot < counts[0], snapshots, jnp.zeros_like(snapshots))
    scale = math.sqrt(slots * lax.axis_size("row"))
    whole = lax.all_gather(live, "snap", axis=0, tiled=True)
    gram = lax.psum(gram_of(whole), "row")
    r_factor, weights = factors(gram, scale)
    start = lax.axis_index("snap") * narrow
    own_weights = lax.dynamic_slice_in_dim(weights, start, narrow, 1)
    basis = apply_weights(own_weights, whole)
    return (basis, r_factor)


def mxu_nt(a, b):
    return lax.dot_general(
        a, b, (((1,), (1,)), ((), ())), preferred_element_type=jnp.float32
    )


def partial_kernel(
    pieces, counts_ref, x_ref, part_ref, first_ref, later_ref, last_ref,
    own, got, mine, near, summed, theirs,
    load_sem, send_sem, recv_sem, keep_sem, back_sem, sum_send, sum_recv, near_send, near_recv,
):
    snap = lax.axis_index("snap")
    core = lax.rem(lax.axis_index("row"), 2)
    other = {"snap": 1 - snap}
    pair = {"row": lax.axis_index("row") + 1 - 2 * core}
    narrow, slots = x_ref.shape
    half = slots // 2
    step = half // pieces
    count = counts_ref[0]

    barrier = pltpu.get_barrier_semaphore()
    pl.semaphore_signal(barrier, inc=1, device_id=other, device_id_type=MESH)
    pl.semaphore_signal(barrier, inc=1, device_id=pair, device_id_type=MESH)

    loads = []
    for c in range(2 * pieces):
        at = pl.ds(c * step, step)
        copy = pltpu.make_async_copy(x_ref.at[:, at], own.at[:, at], load_sem.at[c])
        copy.start()
        loads.append(copy)

    pl.semaphore_wait(barrier, 2)

    def send(i, src, into, dst, size):
        copy = pltpu.make_async_remote_copy(
            src_ref=x_ref.at[:, pl.ds(src, size)],
            dst_ref=into.at[:, pl.ds(dst, size)],
            send_sem=send_sem.at[i],
            recv_sem=recv_sem.at[i],
            device_id=other,
            device_id_type=MESH,
        )
        copy.start()
        return copy

    sends = [
        send(c, pl.multiple_of(snap * half + c * step, step), got, c * step, step)
        for c in range(pieces)
    ]

    def masked(block, start):
        lane = lax.broadcasted_iota(jnp.int32, block.shape, 1) + start
        return jnp.where(lane < count, block, jnp.zeros_like(block))

    total = jnp.zeros((narrow, narrow), jnp.float32)
    for c in range(2 * pieces):
        loads[c].wait()
        block = own[:, c * step:(c + 1) * step]
        total = total + mxu_nt(masked(block, c * step), block)
    mine[0] = total
    keeps = []
    start = first_ref.shape[1]
    for i, ref in enumerate((later_ref, last_ref)):
        size = ref.shape[1]
        keep = pltpu.make_async_copy(own.at[:, pl.ds(start, size)], ref, keep_sem.at[i])
        keep.start()
        keeps.append(keep)
        start += size

    rows = narrow // 2

    def sum_copy(i):
        away = pltpu.make_async_remote_copy(
            src_ref=mine.at[i, pl.ds(pl.multiple_of((1 - core) * rows, SUBLANES), rows)],
            dst_ref=near.at[i],
            send_sem=near_send.at[i],
            recv_sem=near_recv.at[i],
            device_id=pair,
            device_id_type=MESH,
        )
        away.start()
        away.wait()
        kept = mine[i, pl.ds(pl.multiple_of(core * rows, SUBLANES), rows), :]
        summed[i] = kept + near[i]
        return pltpu.make_async_remote_copy(
            src_ref=summed.at[i],
            dst_ref=theirs.at[i],
            send_sem=sum_send.at[i],
            recv_sem=sum_recv.at[i],
            device_id=other,
            device_id_type=MESH,
        )

    diagonal = sum_copy(0)
    diagonal.start()
    spare = first_ref.shape[1] - half
    ahead = spare * 3 // 4
    extras = [send(pieces, half, first_ref, half, ahead)]

    cross = jnp.zeros((narrow, narrow), jnp.float32)
    backs = []
    base = (1 - snap) * half
    for c in range(pieces):
        sends[c].wait_recv()
        here = pl.ds(c * step, step)
        back = pltpu.make_async_copy(got.at[:, here], first_ref.at[:, here], back_sem.at[c])
        back.start()
        backs.append(back)
        start = pl.multiple_of(base + c * step, step)
        block = masked(own[:, pl.ds(start, step)], start)
        cross = cross + mxu_nt(block, got[:, c * step:(c + 1) * step])
    mine[1] = jnp.where(snap == 0, cross, cross.T)
    crossed = sum_copy(1)
    crossed.start()
    at = half + ahead
    extras.append(send(pieces + 1, at, first_ref, at, spare - ahead))
    for copy in sends:
        copy.wait_send()
    for copy in keeps:
        copy.wait()
    diagonal.wait()
    part_ref[0:rows, :] = jnp.where(snap == 0, summed[0], theirs[0])
    part_ref[rows:2 * rows, :] = jnp.where(snap == 0, theirs[0], summed[0])
    crossed.wait()
    part_ref[2 * rows:3 * rows, :] = summed[1] + theirs[1]
    for copy in extras:
        copy.wait()
    for copy in backs:
        copy.wait()


def partial_grams(snapshots, counts, pieces=8):
    narrow, slots = snapshots.shape
    half = slots // 2
    step = half // pieces
    early = half + step
    last = step
    later = slots - early - last
    any_space = pl.BlockSpec(memory_space=pl.ANY)
    return pl.pallas_call(
        functools.partial(partial_kernel, pieces),
        name="partial_grams",
        out_shape=(
            jax.ShapeDtypeStruct((3 * narrow // 2, narrow), jnp.float32),
            jax.ShapeDtypeStruct((narrow, early), snapshots.dtype),
            jax.ShapeDtypeStruct((narrow, later), snapshots.dtype),
            jax.ShapeDtypeStruct((narrow, last), snapshots.dtype),
        ),
        in_specs=[
            pl.BlockSpec(memory_space=pltpu.SMEM),
            pl.BlockSpec(memory_space=pltpu.HBM),
        ],
        out_specs=(pl.BlockSpec(memory_space=pltpu.VMEM), any_space, any_space, any_space),
        scratch_shapes=[
            pltpu.VMEM((narrow, slots), snapshots.dtype),
            pltpu.VMEM((narrow, half), snapshots.dtype),
            pltpu.VMEM((2, narrow, narrow), jnp.float32),
            pltpu.VMEM((2, narrow // 2, narrow), jnp.float32),
            pltpu.VMEM((2, narrow // 2, narrow), jnp.float32),
            pltpu.VMEM((2, narrow // 2, narrow), jnp.float32),
            pltpu.SemaphoreType.DMA((2 * pieces,)),
            pltpu.SemaphoreType.DMA((pieces + 2,)),
            pltpu.SemaphoreType.DMA((pieces + 2,)),
            pltpu.SemaphoreType.DMA((2,)),
            pltpu.SemaphoreType.DMA((pieces,)),
            pltpu.SemaphoreType.DMA((2,)),
            pltpu.SemaphoreType.DMA((2,)),
            pltpu.SemaphoreType.DMA((2,)),
            pltpu.SemaphoreType.DMA((2,)),
        ],
        compiler_params=pltpu.CompilerParams(
            collective_id=0, has_side_effects=True, vmem_limit_bytes=62 << 20
        ),
    )(counts, snapshots)


def reduce_kernel(n, part_ref, out_ref, parts, send_sem, recv_sem, out_send, out_recv):
    me = lax.axis_index("row")
    core, chip = lax.rem(me, 2), lax.div(me, 2)
    chips = n // 2
    rows = part_ref.shape[0] // chips
    barrier = pltpu.get_barrier_semaphore()
    for d in range(1, n):
        peer = lax.rem(me + d, n)
        pl.semaphore_signal(barrier, inc=1, device_id={"row": peer}, device_id_type=MESH)
    pl.semaphore_wait(barrier, n - 1)

    def at(i):
        return pl.ds(pl.multiple_of(i * rows, SUBLANES), rows)

    copies = []
    for d in range(1, chips):
        peer = lax.rem(chip + d, chips)
        copy = pltpu.make_async_remote_copy(
            src_ref=part_ref.at[at(peer)],
            dst_ref=parts.at[d - 1],
            send_sem=send_sem.at[d - 1],
            recv_sem=recv_sem.at[d - 1],
            device_id={"row": 2 * peer + core},
            device_id_type=MESH,
        )
        copy.start()
        copies.append(copy)
    total = part_ref[at(chip), :]
    for d in range(1, chips):
        copies[d - 1].wait_recv()
        total = total + parts[d - 1]
    out_ref[core, at(chip), :] = total
    results = []
    for d in range(1, n):
        peer = lax.rem(me + d, n)
        copy = pltpu.make_async_remote_copy(
            src_ref=out_ref.at[core, at(chip)],
            dst_ref=out_ref.at[core, at(chip)],
            send_sem=out_send.at[d - 1],
            recv_sem=out_recv.at[d - 1],
            device_id={"row": peer},
            device_id_type=MESH,
        )
        copy.start()
        results.append(copy)
    for copy in copies:
        copy.wait_send()
    for copy in results:
        copy.wait()


def reduce_rows(part):
    n = lax.axis_size("row")
    chips = n // 2
    rows = part.shape[0] // chips
    vmem = pl.BlockSpec(memory_space=pltpu.VMEM)
    return pl.pallas_call(
        functools.partial(reduce_kernel, n),
        name="reduce_rows",
        out_shape=jax.ShapeDtypeStruct((2, *part.shape), part.dtype),
        in_specs=[vmem],
        out_specs=vmem,
        scratch_shapes=[
            pltpu.VMEM((chips - 1, rows, part.shape[1]), part.dtype),
            pltpu.SemaphoreType.DMA((chips - 1,)),
            pltpu.SemaphoreType.DMA((chips - 1,)),
            pltpu.SemaphoreType.DMA((n - 1,)),
            pltpu.SemaphoreType.DMA((n - 1,)),
        ],
        compiler_params=pltpu.CompilerParams(
            collective_id=1, has_side_effects=True, vmem_limit_bytes=8 << 20
        ),
        cost_estimate=pl.CostEstimate(
            flops=1 << 30, bytes_accessed=48 << 20, transcendentals=0
        ),
    )(part)


def eliminate(groups):
    shape = groups[0].shape
    tall = shape[0]
    lane = lax.broadcasted_iota(jnp.int32, shape, 1)
    sub = lax.broadcasted_iota(jnp.int32, shape, 0)
    groups = list(groups)
    count = len(groups)

    def line(block, p):
        return jnp.broadcast_to(block[p:p + 1, :], shape)

    for g in range(count):
        columns = [
            [
                jnp.broadcast_to(groups[v][:, g * tall + q:g * tall + q + 1], shape)
                for v in range(g, count)
            ]
            for q in range(tall)
        ]
        for p in range(tall):
            here = lane == g * tall + p
            pivot = line(columns[p][0], p)
            root = lax.rsqrt(pivot)
            root = root * (1.5 - 0.5 * pivot * root * root)
            lefts = [column * root for column in columns[p]]
            lefts[0] = jnp.where(sub > p, lefts[0], 0.0)
            for q in range(p + 1, tall):
                top = line(columns[q][0], p) * root
                columns[q] = [c - m * top for c, m in zip(columns[q], lefts)]
            row = jnp.where(here, root, line(groups[g], p) * root)
            for v in range(g, count):
                old = groups[v]
                new = jnp.where(here, 0.0, old) - lefts[v - g] * row
                if v == g:
                    new = jnp.where(sub == p, row, jnp.where(sub > p, new, old))
                groups[v] = new
    return groups


def factor_kernel(scale, gram_ref, r_ref, own_ref, other_ref, work, roots):
    narrow = gram_ref.shape[2]
    rows = narrow // 2
    snap = lax.axis_index("snap")
    row = lax.broadcasted_iota(jnp.int32, (narrow, narrow), 0)
    col = lax.broadcasted_iota(jnp.int32, (narrow, narrow), 1)

    def gram(i):
        here = slice(i * rows, (i + 1) * rows)
        return jnp.concatenate([gram_ref[0, here, :], gram_ref[1, here, :]], axis=0)

    def dot(a, b, dims):
        return lax.dot_general(
            a, b, (dims, ((), ())), precision=HIGH, preferred_element_type=jnp.float32
        )

    def diagonal(which):
        full = work[which]
        inverse = jnp.where(col <= row, full, 0.0)
        upper = jnp.where(col > row, full, 0.0)
        upper = jnp.where(col == row, 1.0 / full, upper)
        return inverse, upper

    work[0] = gram(0)
    work[1] = gram(1)

    @pl.loop(0, 2)
    def _(block):
        groups = [
            work[block, SUBLANES * v:SUBLANES * (v + 1), :] for v in range(narrow // SUBLANES)
        ]
        for v, group in enumerate(eliminate(groups)):
            work[block, SUBLANES * v:SUBLANES * (v + 1), :] = group

        @pl.when(block == 0)
        def _():
            inverse, _ = diagonal(0)
            right = dot(inverse, gram(2), ((1,), (0,)))
            roots[...] = right
            work[1] = work[1] - dot(right, right, ((0,), (0,)))

    inverse0, upper0 = diagonal(0)
    inverse1, upper1 = diagonal(1)
    right = roots[...]
    below = -dot(inverse1, dot(right, inverse0, ((0,), (0,))), ((1,), (0,)))
    r_ref[0:narrow, 0:narrow] = upper0 / scale
    r_ref[0:narrow, narrow:] = right / scale
    r_ref[narrow:, 0:narrow] = jnp.zeros_like(right)
    r_ref[narrow:, narrow:] = upper1 / scale
    own = jnp.where(snap == 0, inverse0, inverse1)
    own_ref[...] = (own * scale).astype(own_ref.dtype)
    other = jnp.where(snap == 0, 0.0, below)
    other_ref[...] = (other * scale).astype(other_ref.dtype)


def factor(gram, scale, dtype):
    narrow = gram.shape[2]
    vmem = pl.BlockSpec(memory_space=pltpu.VMEM)
    return pl.pallas_call(
        functools.partial(factor_kernel, scale),
        name="factor",
        out_shape=(
            jax.ShapeDtypeStruct((2 * narrow, 2 * narrow), jnp.float32),
            jax.ShapeDtypeStruct((narrow, narrow), dtype),
            jax.ShapeDtypeStruct((narrow, narrow), dtype),
        ),
        in_specs=[vmem],
        out_specs=(vmem, vmem, vmem),
        scratch_shapes=[
            pltpu.VMEM((2, narrow, narrow), jnp.float32),
            pltpu.VMEM((narrow, narrow), jnp.float32),
        ],
        compiler_params=pltpu.CompilerParams(vmem_limit_bytes=8 << 20),
        cost_estimate=pl.CostEstimate(
            flops=1 << 30, bytes_accessed=96 << 20, transcendentals=0
        ),
    )(gram)


def basis_kernel(
    pieces, first_piece, counts_ref, own_w, other_w, own_ref, got_ref, *rest
):
    out_ref, stage, sems = rest[-3:]
    narrow, width = got_ref.shape
    step = width // pieces
    count = counts_ref[0]
    weights = jnp.concatenate([own_w[...], other_w[...]], axis=1)
    copies = []
    for c in range(pieces):
        here = pl.ds(c * step, step)
        start = first_piece + c * step
        both = jnp.concatenate(
            [own_ref[:, start:start + step], got_ref[:, c * step:(c + 1) * step]], axis=0
        )
        value = lax.dot_general(
            weights, both, (((1,), (0,)), ((), ())), preferred_element_type=jnp.float32
        )
        lane = lax.broadcasted_iota(jnp.int32, value.shape, 1) + start
        stage[:, c * step:(c + 1) * step] = jnp.where(lane < count, value, 0.0).astype(stage.dtype)
        copy = pltpu.make_async_copy(
            stage.at[:, here], out_ref.at[:, pl.ds(start, step)], sems.at[c]
        )
        copy.start()
        copies.append(copy)
    for copy in copies:
        copy.wait()


def form_basis(counts, own_w, other_w, snapshots, got, start, before=None, most=2048):
    narrow, width = got.shape
    pieces = next(n for n in range(1, width) if width % (n * LANES) == 0 and width // n <= most)
    vmem = pl.BlockSpec(memory_space=pltpu.VMEM)
    hbm = pl.BlockSpec(memory_space=pltpu.HBM)
    operands = [counts, own_w, other_w, snapshots, got]
    specs = [pl.BlockSpec(memory_space=pltpu.SMEM), vmem, vmem, vmem, vmem]
    aliases = {}
    if before is not None:
        aliases = {len(operands): 0}
        operands.append(before)
        specs.append(hbm)
    return pl.pallas_call(
        functools.partial(basis_kernel, pieces, start),
        name="form_basis",
        out_shape=jax.ShapeDtypeStruct(snapshots.shape, snapshots.dtype),
        in_specs=specs,
        out_specs=hbm,
        input_output_aliases=aliases,
        scratch_shapes=[
            pltpu.VMEM((narrow, width), snapshots.dtype),
            pltpu.SemaphoreType.DMA((pieces,)),
        ],
        compiler_params=pltpu.CompilerParams(vmem_limit_bytes=16 << 20),
        cost_estimate=pl.CostEstimate(
            flops=4 * narrow * narrow * width,
            bytes_accessed=8 * narrow * width,
            transcendentals=0,
        ),
    )(*operands)


def halves(snapshots, counts):
    slots = snapshots.shape[1]
    scale = math.sqrt(slots * lax.axis_size("row"))
    part, *got = partial_grams(snapshots, counts)
    got[1:] = [lax.ppermute(piece, "snap", [(0, 1)]) for piece in got[1:]]
    gram = reduce_rows(part)
    r_factor, own_w, other_w = factor(gram, scale, snapshots.dtype)
    basis, start = None, 0
    for piece in got:
        basis = form_basis(counts, own_w, other_w, snapshots, piece, start, basis)
        start += piece.shape[1]
    return (basis, r_factor)


def two_halves(mesh):
    return mesh.shape["snap"] == 2 and mesh.shape["row"] == 16


def solution(mesh):
    placed = (P("snap", "row"), P("row"))
    body = halves if two_halves(mesh) else shards
    return jax.shard_map(
        body, mesh=mesh, in_specs=placed, out_specs=(P("snap", "row"), P()), check_vma=False
    )
```
